256 devices in a mesh: cuts: 16 (over y, x_lo, core), pencil: 16 (over z, x_hi).
Axes of the slice: x: 4 (x_hi: 2, x_lo: 2; x = x_hi * 2 + x_lo), y: 4, z: 8, core: 2. Of those that a mesh axis runs over, the one named last changes fastest.
Arguments:
- wavefunctions: bfloat16 [64, 9216, 192], P('cuts', 'pencil'), may hold values from -8 to 8
- potential: float32 [192, 192, 192], P('pencil'), may hold values from -6 to 6
- keep_mask: int32 [16, 2, 2], P('cuts'), may hold values 0 or 1
- stick_map: int32 [9216], P('pencil'), may hold values from 0 to 575, as said below
Outputs:
- hamiltonian_bands: bfloat16 [64, 9216, 192], P('cuts', 'pencil')
The draws below stay inside these ranges and needn't reach their ends.
Inputs may be any that keep to these rules, and one draw needn't show every extreme that they name: `stick_map`: each block of 576 consecutive entries (one index of pencil) is a permutation of 0 to 575.
All inputs are finite; a program needn't handle non-finite values. No bound on the sum of `keep_mask` on one device may be relied on, other than what follows from the above.
Results may differ from the reference program's by a relative error of at most 0.0065.
Values may be sent and summed in bfloat16 or wider, within the bound.
No kernel may reach another device: no remote copies, remote signals or barrier semaphores. Data moves between devices by JAX's collectives and lax.ppermute only.
A program may use at most 128 MiB of HBM per device.

```python
import math
import jax
import jax.numpy as jnp
from jax import lax

GRID = 192
EDGE = 2
BANDS_DEV = 4
GBOX = 96
BANDS = 64
GY_DEV = 6
STICKS = 9216
STICKS_DEV = 576
N_CUTS = 16


def fresh_noise(noise_key, band_index):
    band_key = jax.random.fold_in(noise_key, band_index)
    return jax.random.normal(band_key, (STICKS, 2 * GBOX), jnp.float32)


def draw_wavefunctions(key, part):
    blocks = STICKS // STICKS_DEV
    coef_key = jax.random.fold_in(key, 11)
    sign_key = jax.random.fold_in(key, 12)
    scale_key = jax.random.fold_in(key, 13)
    noise_key = jax.random.fold_in(key, 14)
    magnitudes = jax.random.uniform(coef_key, (BANDS, blocks), jnp.float32, 0.3, 0.95)
    signs = (2 * jax.random.randint(sign_key, (BANDS, blocks), 0, 2) - 1).astype(jnp.float32)
    coefficients = jnp.repeat(magnitudes * signs, STICKS_DEV, axis=1)
    block_scale = jnp.exp(jax.random.uniform(scale_key, (blocks,), jnp.float32, 0.0, math.log(3.0))) / math.sqrt(3.0)
    block_scale = jnp.repeat(block_scale, STICKS_DEV)

    def advance(previous, inputs):
        band_index, coef_row = inputs
        column = coef_row[:, None]
        following = column * previous + jnp.sqrt(1.0 - column * column) * fresh_noise(noise_key, band_index)
        return (following, following)
    start = fresh_noise(noise_key, BANDS)
    band_ids = jnp.arange(BANDS, dtype=jnp.int32)
    unused, mixture = lax.scan(advance, start, (band_ids, coefficients))
    mixture = mixture * block_scale[None, :, None]
    return jnp.clip(mixture, -8.0, 8.0).astype(jnp.bfloat16)


def draw_stick_map(key, part):
    owners = STICKS // STICKS_DEV
    key_list = jax.random.split(key, owners)
    orders = jax.vmap(lambda single: jax.random.permutation(single, STICKS_DEV))(key_list)
    return orders.reshape(STICKS).astype(jnp.int32)


def with_ends(drawn, key, least, high):
    longest = drawn.shape.index(max(drawn.shape))
    spots = []
    for shift in (0, 1):
        where = [jax.random.randint(jax.random.fold_in(key, axis), (), 0, length) for axis, length in enumerate(drawn.shape)]
        where[longest] = (where[longest] + shift) % drawn.shape[longest]
        spots.append(tuple(where))
    return drawn.at[spots[0]].set(least).at[spots[1]].set(high)


def shard_levels(stream_key, extent, cuts, low, high):
    factor_of, own = 1.0, jax.random.fold_in(stream_key, 6)
    for dim, shards_of in cuts:
        draws = jnp.exp(jax.random.uniform(jax.random.fold_in(own, dim), (shards_of,), jnp.float32, low / len(cuts), high / len(cuts)))
        factor_of = factor_of * jnp.repeat(draws, extent[dim] // shards_of).reshape([-1 if axis == dim else 1 for axis in range(len(extent))])
    return factor_of


def normal_values(key, shape, scale, limit, cuts=(), held_as=jnp.bfloat16):
    level = shard_levels(key, shape, cuts, -0.22, 0.18) if cuts else 1.0
    array = jax.random.normal(key, shape, jnp.float32) * scale * level
    return jnp.minimum(jnp.maximum(array, -limit), limit).astype(held_as)


def setup_inputs(seed: int = 0) -> dict:
    key_of = jax.random.split(jax.random.key(seed), 5)
    wavefunctions = draw_wavefunctions(jax.random.fold_in(key_of[4], 71), 0)
    potential = normal_values(key_of[1], (GRID, GRID, GRID), 1.0, 6.0, ((0, 16),), jnp.float32)
    keep_mask = with_ends((jax.random.randint(key_of[2], (N_CUTS, EDGE, EDGE), 0, 2) < 1).astype(jnp.int32), jax.random.fold_in(key_of[2], 1), 0, 1)
    stick_map = draw_stick_map(jax.random.fold_in(key_of[4], 71), 0)
    return {"wavefunctions": wavefunctions, "potential": potential, "keep_mask": keep_mask, "stick_map": stick_map}


def dft_tables(box_size, length):
    frequency = jnp.arange(box_size, dtype=jnp.float32) - float(box_size // 2)
    points = jnp.arange(length, dtype=jnp.float32)
    phases = 2.0 * math.pi / length * jnp.mod(frequency[:, None] * points[None, :], float(length))
    ahead_scale = 1.0 / math.sqrt(box_size)
    behind_scale = math.sqrt(box_size) / length
    ahead_cos = (jnp.cos(phases) * ahead_scale).astype(jnp.bfloat16)
    ahead_sin = (jnp.sin(phases) * ahead_scale).astype(jnp.bfloat16)
    behind_cos = (jnp.cos(phases).T * behind_scale).astype(jnp.bfloat16)
    behind_sin = (-jnp.sin(phases).T * behind_scale).astype(jnp.bfloat16)
    return (ahead_cos, ahead_sin, behind_cos, behind_sin)

def last_matrix(cos_table, sin_table):
    upper_rows = jnp.concatenate([cos_table, sin_table], axis=1)
    lower_rows = jnp.concatenate([-sin_table, cos_table], axis=1)
    return jnp.concatenate([upper_rows, lower_rows], axis=0)

def combine_halves(cos_part, sin_part):
    middle = cos_part.shape[-1] // 2
    real_part = cos_part[..., :middle] - sin_part[..., middle:]
    imag_part = sin_part[..., :middle] + cos_part[..., middle:]
    return jnp.concatenate([real_part, imag_part], axis=-1)

def along_axis(values, cos_table, sin_table, pattern):
    operand = values.astype(jnp.float32)
    cos_part = jnp.einsum(pattern, operand, cos_table.astype(jnp.float32), precision=lax.Precision.HIGHEST)
    sin_part = jnp.einsum(pattern, operand, sin_table.astype(jnp.float32), precision=lax.Precision.HIGHEST)
    return combine_halves(cos_part, sin_part)

def along_last(values, matrix):
    return jnp.einsum('abc,cd->abd', values.astype(jnp.float32), matrix.astype(jnp.float32), precision=lax.Precision.HIGHEST)

def kinetic_table(box_size, row_start, column_count):
    center = box_size // 2
    freq_rows = jnp.arange(box_size, dtype=jnp.float32) - center
    freq_cols = (row_start + jnp.arange(column_count, dtype=jnp.int32)).astype(jnp.float32) - center
    freq_depth = jnp.arange(box_size, dtype=jnp.float32) - center
    freq_depth = jnp.concatenate([freq_depth, freq_depth])
    squares = freq_rows[:, None, None] ** 2 + freq_cols[None, :, None] ** 2 + freq_depth[None, None, :] ** 2
    return 0.5 * squares / float(center * center)

def reference(wavefunctions, potential, keep_mask, stick_map):
    row_width = 2 * GBOX
    middle = GBOX
    precise = lax.Precision.HIGHEST
    slices = wavefunctions.reshape(N_CUTS, BANDS_DEV, STICKS, row_width)
    lower_edge = slices[:, :EDGE].astype(jnp.float32)
    upper_edge = slices[:, BANDS_DEV - EDGE:].astype(jnp.float32)
    neighbor = jnp.concatenate([jnp.zeros_like(upper_edge[:1]), upper_edge[:-1]], axis=0)
    correlation_real = jnp.einsum('sjgc,sigc->sji', neighbor, lower_edge, precision=precise)
    correlation_imag = jnp.einsum('sjgc,sigc->sji', neighbor[..., :middle], lower_edge[..., middle:], precision=precise) - jnp.einsum('sjgc,sigc->sji', neighbor[..., middle:], lower_edge[..., :middle], precision=precise)
    neighbor_norms = lax.optimization_barrier(jnp.sum(neighbor * neighbor, axis=(2, 3)))
    divisor = neighbor_norms[:, None, :] + 1e-05
    keep_factor = keep_mask.astype(jnp.float32)
    weight_real = keep_factor * jnp.transpose(correlation_real, (0, 2, 1)) / divisor
    weight_imag = keep_factor * jnp.transpose(correlation_imag, (0, 2, 1)) / divisor
    cos_part = jnp.einsum('sij,sjgc->sigc', weight_real, neighbor, precision=precise)
    sin_part = jnp.einsum('sij,sjgc->sigc', weight_imag, neighbor, precision=precise)
    new_lower = (lower_edge - combine_halves(cos_part, sin_part)).astype(jnp.bfloat16)
    ortho = slices.at[:, :EDGE].set(new_lower).reshape(BANDS, STICKS, row_width)
    owner_rows = jnp.arange(STICKS, dtype=jnp.int32) // STICKS_DEV
    freq_first = stick_map // GY_DEV
    freq_second = owner_rows * GY_DEV + stick_map % GY_DEV
    position = (freq_first * GBOX + freq_second).astype(jnp.int32)
    inverse = jnp.zeros((STICKS,), jnp.int32).at[position].set(jnp.arange(STICKS, dtype=jnp.int32))
    kinetic = kinetic_table(GBOX, 0, GBOX)
    ahead_cos, ahead_sin, behind_cos, behind_sin = dft_tables(GBOX, GRID)
    ahead_last = last_matrix(ahead_cos, ahead_sin)
    behind_last = last_matrix(behind_cos, behind_sin)
    doubled = jnp.concatenate([potential, potential], axis=-1)

    def one_band(band_rows):
        freq_block = band_rows[inverse].reshape(GBOX, GBOX, row_width)
        section_one = along_axis(freq_block, ahead_cos, ahead_sin, 'kyc,kn->nyc').astype(jnp.bfloat16)
        section_two = along_last(section_one, ahead_last).astype(jnp.bfloat16)
        real_space = along_axis(section_two, ahead_cos, ahead_sin, 'xkc,kn->xnc').astype(jnp.bfloat16)
        scaled = (doubled * real_space.astype(jnp.float32)).astype(jnp.bfloat16)
        back_one = along_axis(scaled, behind_cos, behind_sin, 'xnc,nk->xkc').astype(jnp.bfloat16)
        back_two = along_last(back_one, behind_last).astype(jnp.bfloat16)
        back_three = along_axis(back_two, behind_cos, behind_sin, 'nyc,nk->kyc')
        result = (back_three + kinetic * freq_block.astype(jnp.float32)).astype(jnp.bfloat16)
        return result.reshape(STICKS, row_width)[position]
    return lax.map(one_band, ortho)
```

```python
import math

import jax
import jax.numpy as jnp
import ml_dtypes
import numpy as np
from jax import lax
from jax.experimental import pallas as pl
from jax.experimental.pallas import tpu as pltpu
from jax.sharding import PartitionSpec as P

GRID = 192
EDGE = 2
GBOX = 96
PENCILS = 16
X_DEV = GRID // PENCILS
GY_DEV = GBOX // PENCILS
STICKS_DEV = GBOX * GY_DEV
WIDTH = 2 * GBOX
CHUNK = X_DEV * GY_DEV
ROWS = PENCILS * CHUNK
LANES = EDGE * WIDTH
BLOCK = 4 * CHUNK
STATS = 16

bf16 = jnp.bfloat16
f32 = jnp.float32
NT = (((1,), (1,)), ((), ()))
TN = (((0,), (0,)), ((), ()))
VMEM = pltpu.VMEM


def tables():
    phases = 2.0 * np.pi / GRID * np.mod(np.outer(np.arange(GBOX) - GBOX // 2, np.arange(GRID)), GRID)
    scale = 1.0 / math.sqrt(GBOX)
    rounded = lambda a: a.astype(np.float32).astype(ml_dtypes.bfloat16).astype(np.float64)
    return rounded(np.cos(phases) * scale), rounded(np.sin(phases) * scale)


def constants():
    cos, sin = tables()
    low = lambda a: np.asarray(a, np.float32).astype(ml_dtypes.bfloat16)
    order = (np.arange(PENCILS)[:, None, None] * X_DEV + np.zeros((1, GY_DEV, 1), int) + np.arange(X_DEV)[None, None, :]).reshape(-1)
    first = np.concatenate([cos.T[order], sin.T[order]], axis=0)
    core = np.zeros((WIDTH, 512))
    core[:GBOX, :GRID] = cos
    core[GBOX:, :GRID] = -sin
    core[:GBOX, 256 : 256 + GRID] = sin
    core[GBOX:, 256 : 256 + GRID] = cos
    third = np.zeros((2, 256, 512))
    third[0, :WIDTH] = core
    third[1, 64:] = core
    second = np.block([[cos.T, -sin.T], [sin.T, cos.T]])
    back_second = 0.5 * np.block([[cos, sin], [-sin, cos]])
    back = 0.5 * np.block([[cos.T, -sin.T], [sin.T, cos.T]])
    back_third = np.zeros((2, 2 * GRID, 256))
    back_third[0, :, :WIDTH] = back
    back_third[1, :, 64:] = back
    return [low(a) for a in (first, third, second, back_second, back_third)]


def dot(a, b, dims=None):
    if dims is None:
        return jnp.dot(a, b, preferred_element_type=f32)
    return lax.dot_general(a, b, dims, preferred_element_type=f32)


def whole(*_):
    return pl.BlockSpec(memory_space=VMEM)


def sixth(value):
    return (value * 10923) >> 16


def matrix_kernel(map_ref, first_ref, cos_ref, sin_ref):
    position = map_ref[...]
    kx = sixth(position)
    ky = position - GY_DEV * kx
    select = (lax.broadcasted_iota(jnp.int32, (GBOX, STICKS_DEV), 0) == kx).astype(f32).astype(bf16)
    row = lax.broadcasted_iota(jnp.int32, (CHUNK, STICKS_DEV), 0)
    row_ky = (row * 5462) >> 16
    mask = row_ky == ky
    for part in range(2):
        out_ref = (cos_ref, sin_ref)[part]
        for b in range(PENCILS):
            spread = dot(first_ref[pl.ds(part * ROWS + b * CHUNK, CHUNK), :], select)
            out_ref[pl.ds(b * CHUNK, CHUNK), :] = jnp.where(mask, spread, 0.0).astype(bf16)


def build_matrix(position, first):
    shape = jax.ShapeDtypeStruct((ROWS, STICKS_DEV), bf16)
    return pl.pallas_call(
        matrix_kernel,
        out_shape=(shape, shape),
        in_specs=[whole(), whole()],
        out_specs=(whole(), whole()),
        name="matrix",
    )(position, first)


def stats_kernel(upper_ref, lower_ref, out_ref):
    def total(a, b):
        return jnp.sum(a * b)

    rows = lax.broadcasted_iota(jnp.int32, (STATS, 128), 0)
    out = jnp.zeros((STATS, 128), f32)
    for j in range(EDGE):
        p_re = upper_ref[j, :GBOX, :].astype(f32)
        p_im = upper_ref[j, GBOX:, :].astype(f32)
        for i in range(EDGE):
            u_re = lower_ref[i, :GBOX, :].astype(f32)
            u_im = lower_ref[i, GBOX:, :].astype(f32)
            real = jnp.sum(p_re * u_re + p_im * u_im)
            imag = jnp.sum(p_re * u_im - p_im * u_re)
            out = jnp.where(rows == 2 * j + i, real, out)
            out = jnp.where(rows == 4 + 2 * j + i, imag, out)
        out = jnp.where(rows == 8 + j, jnp.sum(p_re * p_re + p_im * p_im), out)
    out_ref[...] = out


def stats(upper, lower):
    return pl.pallas_call(
        stats_kernel,
        out_shape=jax.ShapeDtypeStruct((STATS, 128), f32),
        in_specs=[whole(), whole()],
        out_specs=whole(),
        name="stats",
    )(upper, lower)


def spread_rows(bands, cos_ref, sin_ref, out_ref):
    plain = jnp.concatenate([part for re, im in bands for part in (re, im)], axis=0)
    turned = jnp.concatenate([part for re, im in bands for part in (-im, re)], axis=0)
    for b in range(0, ROWS, BLOCK):
        rows = pl.ds(b, BLOCK)
        out_ref[rows, :] = (dot(cos_ref[rows, :], plain, NT) + dot(sin_ref[rows, :], turned, NT)).astype(bf16)


def ahead_kernel(bands_ref, cos_ref, sin_ref, out_ref):
    spread_rows([(bands_ref[b, :GBOX, :], bands_ref[b, GBOX:, :]) for b in range(EDGE)], cos_ref, sin_ref, out_ref)


def ahead(bands, cos, sin):
    return pl.pallas_call(
        ahead_kernel,
        out_shape=jax.ShapeDtypeStruct((ROWS, LANES), bf16),
        grid=(1,),
        in_specs=[pl.BlockSpec((EDGE, WIDTH, STICKS_DEV), lambda i: (1, 0, 0)), whole(), whole()],
        out_specs=whole(),
        name="ahead",
    )(bands, cos, sin)


def edge_kernel(keep_ref, total_ref, bands_ref, upper_ref, cos_ref, sin_ref, out_ref, ortho_ref):
    bands = []
    for i in range(EDGE):
        u_re = bands_ref[i, :GBOX, :].astype(f32)
        u_im = bands_ref[i, GBOX:, :].astype(f32)
        for j in range(EDGE):
            keep = keep_ref[0, i, j].astype(f32)
            divisor = total_ref[8 + j : 9 + j, 0:1] + 1e-05
            w_re = keep * total_ref[2 * j + i : 2 * j + i + 1, 0:1] / divisor
            w_im = keep * total_ref[4 + 2 * j + i : 5 + 2 * j + i, 0:1] / divisor
            p_re = upper_ref[j, :GBOX, :].astype(f32)
            p_im = upper_ref[j, GBOX:, :].astype(f32)
            u_re = u_re - (w_re * p_re - w_im * p_im)
            u_im = u_im - (w_re * p_im + w_im * p_re)
        re, im = u_re.astype(bf16), u_im.astype(bf16)
        ortho_ref[i, :GBOX, :] = re
        ortho_ref[i, GBOX:, :] = im
        bands.append((re, im))
    spread_rows(bands, cos_ref, sin_ref, out_ref)


def edge_ahead(keep, total, bands, upper, cos, sin):
    return pl.pallas_call(
        edge_kernel,
        out_shape=(
            jax.ShapeDtypeStruct((ROWS, LANES), bf16),
            jax.ShapeDtypeStruct((EDGE, WIDTH, STICKS_DEV), bf16),
        ),
        grid=(1,),
        in_specs=[
            pl.BlockSpec(memory_space=pltpu.SMEM),
            whole(),
            pl.BlockSpec((EDGE, WIDTH, STICKS_DEV), lambda i: (0, 0, 0)),
            whole(),
            whole(),
            whole(),
        ],
        out_specs=(whole(), whole()),
        name="edge",
    )(keep, total, bands, upper, cos, sin)


def grid_kernel(rows_ref, potential_ref, third_ref, second_ref, back_second_ref, back_third_ref, out_ref, wide_ref, back_ref):
    for t in range(3):
        wide_ref[t] = rows_ref[:, 128 * t : 128 * t + 128].astype(f32)

    def plane(x, carry):
        rows = pl.ds(x, GBOX, stride=X_DEV)
        section = jnp.concatenate([wide_ref[t, rows, :] for t in range(3)], axis=1).astype(bf16)
        field = potential_ref[x]
        results = []
        for b in range(EDGE):
            lanes = section[:, 128 * b : 128 * b + 256]
            two = dot(lanes, third_ref[b]).astype(bf16)
            stacked = jnp.concatenate([two[:, :GRID], two[:, 256 : 256 + GRID]], axis=0)
            space = dot(second_ref[...], stacked)
            scaled = jnp.concatenate([space[:GRID] * field, space[GRID:] * field], axis=0).astype(bf16)
            one = dot(back_second_ref[...], scaled).astype(bf16)
            results.append(dot(one[:GBOX], back_third_ref[b, :GRID, :]) + dot(one[GBOX:], back_third_ref[b, GRID:, :]))
        back_ref[0, rows, :] = results[0][:, :128]
        back_ref[1, rows, :] = results[0][:, 128:] + results[1][:, :128]
        back_ref[2, rows, :] = results[1][:, 128:]
        return carry

    lax.fori_loop(0, X_DEV, plane, 0)
    for t in range(3):
        out_ref[:, 128 * t : 128 * t + 128] = back_ref[t].astype(bf16)


def on_grid(rows, potential, consts):
    third, second, back_second, back_third = consts
    flops = 2 * EDGE * X_DEV * (96 * 256 * 512 + 384 * 256 * 256 * 2 + 96 * 512 * 256)
    return pl.pallas_call(
        grid_kernel,
        out_shape=jax.ShapeDtypeStruct((ROWS, LANES), bf16),
        in_specs=[whole()] * 6,
        out_specs=whole(),
        scratch_shapes=[VMEM((3, ROWS, 128), f32), VMEM((3, ROWS, 128), f32)],
        cost_estimate=pl.CostEstimate(flops=flops, bytes_accessed=8_000_000, transcendentals=0),
        name="grid",
    )(rows, potential, third, second, back_second, back_third)


def behind_kernel(map_ref, across_ref, rows_ref, cos_ref, sin_ref, bands_ref, out_ref):
    position = map_ref[...]
    kx = sixth(position)
    gx = (kx - GBOX // 2).astype(f32)
    gy = (position - GY_DEV * kx + GY_DEV * across_ref[0] - GBOX // 2).astype(f32)
    gz = (lax.broadcasted_iota(jnp.int32, (GBOX, STICKS_DEV), 0) - GBOX // 2).astype(f32)
    kinetic = 0.5 * (gx * gx + gy * gy + gz * gz) / float((GBOX // 2) ** 2)
    rows = rows_ref[...]
    by_cos = dot(rows, cos_ref[...], TN)
    by_sin = dot(rows, sin_ref[...], TN)
    for b in range(EDGE):
        re = slice(b * WIDTH, b * WIDTH + GBOX)
        im = slice(b * WIDTH + GBOX, (b + 1) * WIDTH)
        out_ref[b, :GBOX, :] = (0.5 * (by_cos[re] + by_sin[im]) + kinetic * bands_ref[b, :GBOX, :].astype(f32)).astype(bf16)
        out_ref[b, GBOX:, :] = (0.5 * (by_cos[im] - by_sin[re]) + kinetic * bands_ref[b, GBOX:, :].astype(f32)).astype(bf16)


def behind(position, across, rows, cos, sin, bands, index):
    return pl.pallas_call(
        behind_kernel,
        out_shape=jax.ShapeDtypeStruct((EDGE, WIDTH, STICKS_DEV), bf16),
        grid=(1,),
        in_specs=[
            whole(),
            pl.BlockSpec(memory_space=pltpu.SMEM),
            whole(),
            whole(),
            whole(),
            pl.BlockSpec((EDGE, WIDTH, STICKS_DEV), lambda i: (index, 0, 0)),
        ],
        out_specs=whole(),
        name="behind",
    )(position, across, rows, cos, sin, bands)


def exchange(rows):
    blocks = rows.reshape(PENCILS, CHUNK, LANES)
    return lax.all_to_all(blocks, "pencil", split_axis=0, concat_axis=0, tiled=True).reshape(ROWS, LANES)


def total_over_pencil(value):
    for bit in (2, 4, 8, 1):
        value = value + lax.ppermute(value, "pencil", [(i, i ^ bit) for i in range(PENCILS)])
    return value


def local(wavefunctions, potential, keep_mask, stick_map):
    first, *grid_consts = [jnp.asarray(c) for c in constants()]
    bands = jnp.transpose(wavefunctions, (0, 2, 1))
    slices = lax.axis_size("cuts")
    upper = lax.ppermute(bands[EDGE:], "cuts", [(i, i + 1) for i in range(slices - 1)])
    position = stick_map.reshape(1, STICKS_DEV)
    cos, sin = build_matrix(position, first)
    inner_rows = exchange(ahead(bands, cos, sin))
    total = total_over_pencil(stats(upper, bands[:EDGE]))
    edge_rows, ortho = edge_ahead(keep_mask, total, bands, upper, cos, sin)
    edge_rows = exchange(edge_rows)
    inner_back = exchange(on_grid(inner_rows, potential, grid_consts))
    edge_back = exchange(on_grid(edge_rows, potential, grid_consts))
    across = lax.axis_index("pencil").reshape(1).astype(jnp.int32)
    inner_out = behind(position, across, inner_back, cos, sin, bands, 1)
    edge_out = behind(position, across, edge_back, cos, sin, ortho, 0)
    return jnp.transpose(jnp.concatenate([edge_out, inner_out], axis=0), (0, 2, 1))


def solution(mesh):
    return jax.shard_map(
        local,
        mesh=mesh,
        in_specs=(
            P("cuts", "pencil", None),
            P("pencil", None, None),
            P("cuts", None, None),
            P("pencil"),
        ),
        out_specs=P("cuts", "pencil", None),
        check_vma=False,
    )
```

```python
import math

import jax
import jax.numpy as jnp
import ml_dtypes
import numpy as np
from jax import lax
from jax.experimental import pallas as pl
from jax.experimental.pallas import tpu as pltpu
from jax.sharding import PartitionSpec as P

GRID = 192
EDGE = 2
GBOX = 96
PENCILS = 16
X_DEV = GRID // PENCILS
GY_DEV = GBOX // PENCILS
STICKS_DEV = GBOX * GY_DEV
WIDTH = 2 * GBOX
CHUNK = X_DEV * GY_DEV
ROWS = PENCILS * CHUNK
LANES = EDGE * WIDTH
STATS = 16

bf16 = jnp.bfloat16
f32 = jnp.float32
NT = (((1,), (1,)), ((), ()))
TN = (((0,), (0,)), ((), ()))
VMEM = pltpu.VMEM


def tables():
    phases = 2.0 * np.pi / GRID * np.mod(np.outer(np.arange(GBOX) - GBOX // 2, np.arange(GRID)), GRID)
    scale = 1.0 / math.sqrt(GBOX)
    rounded = lambda a: a.astype(np.float32).astype(ml_dtypes.bfloat16).astype(np.float64)
    return rounded(np.cos(phases) * scale), rounded(np.sin(phases) * scale)


def constants():
    cos, sin = tables()
    low = lambda a: np.asarray(a, np.float32).astype(ml_dtypes.bfloat16)
    order = (np.arange(PENCILS)[:, None, None] * X_DEV + np.zeros((1, GY_DEV, 1), int) + np.arange(X_DEV)[None, None, :]).reshape(-1)
    first = np.concatenate([cos.T[order], sin.T[order]], axis=0)
    pair = np.zeros((2, PENCILS, 2, X_DEV, 2, GBOX))
    for k in range(2):
        pair[0, :, k, :, k, :] = cos.T.reshape(PENCILS, X_DEV, GBOX)
        pair[1, :, k, :, k, :] = sin.T.reshape(PENCILS, X_DEV, GBOX)
    pair = np.concatenate(list(pair.reshape(2, 2 * GRID, 2 * GBOX)), axis=1)
    core = np.zeros((WIDTH, 512))
    core[:GBOX, :GRID] = cos
    core[GBOX:, :GRID] = -sin
    core[:GBOX, 256 : 256 + GRID] = sin
    core[GBOX:, 256 : 256 + GRID] = cos
    third = np.zeros((2, 256, 512))
    third[0, :WIDTH] = core
    third[1, 64:] = core
    second = np.block([[cos.T, -sin.T], [sin.T, cos.T]])
    back_second = 0.5 * np.block([[cos, sin], [-sin, cos]])
    back = 0.5 * np.block([[cos.T, -sin.T], [sin.T, cos.T]])
    back_third = np.zeros((2, 2 * GRID, 256))
    back_third[0, :, :WIDTH] = back
    back_third[1, :, 64:] = back
    return [low(a) for a in (first, pair, third, second, back_second, back_third)]


def dot(a, b, dims=None):
    if dims is None:
        return jnp.dot(a, b, preferred_element_type=f32)
    return lax.dot_general(a, b, dims, preferred_element_type=f32)


def whole(*_):
    return pl.BlockSpec(memory_space=VMEM)


def params(mib):
    return pltpu.CompilerParams(vmem_limit_bytes=mib << 20)


def sixth(value):
    return (value * 10923) >> 16


def matrix_kernel(map_ref, first_ref, cos_ref, sin_ref):
    position = map_ref[...]
    kx = sixth(position)
    ky = position - GY_DEV * kx
    select = (lax.broadcasted_iota(jnp.int32, (GBOX, STICKS_DEV), 0) == kx).astype(f32).astype(bf16)
    row = lax.broadcasted_iota(jnp.int32, (CHUNK, STICKS_DEV), 0)
    row_ky = (row * 5462) >> 16
    mask = row_ky == ky
    for part in range(2):
        out_ref = (cos_ref, sin_ref)[part]
        for b in range(PENCILS):
            spread = dot(first_ref[pl.ds(part * ROWS + b * CHUNK, CHUNK), :], select)
            out_ref[pl.ds(b * CHUNK, CHUNK), :] = jnp.where(mask, spread, 0.0).astype(bf16)


def build_matrix(position, first):
    shape = jax.ShapeDtypeStruct((ROWS, STICKS_DEV), bf16)
    return pl.pallas_call(
        matrix_kernel,
        out_shape=(shape, shape),
        in_specs=[whole(), whole()],
        out_specs=(whole(), whole()),
        compiler_params=params(12),
        name="matrix",
    )(position, first)


def stats_kernel(upper_ref, lower_ref, out_ref):
    rows = lax.broadcasted_iota(jnp.int32, (STATS, 128), 0)
    out = jnp.zeros((STATS, 128), f32)
    for j in range(EDGE):
        p_re = upper_ref[j, :GBOX, :].astype(f32)
        p_im = upper_ref[j, GBOX:, :].astype(f32)
        for i in range(EDGE):
            u_re = lower_ref[i, :GBOX, :].astype(f32)
            u_im = lower_ref[i, GBOX:, :].astype(f32)
            real = jnp.sum(p_re * u_re + p_im * u_im)
            imag = jnp.sum(p_re * u_im - p_im * u_re)
            out = jnp.where(rows == 2 * j + i, real, out)
            out = jnp.where(rows == 4 + 2 * j + i, imag, out)
        out = jnp.where(rows == 8 + j, jnp.sum(p_re * p_re + p_im * p_im), out)
    out_ref[...] = out


def stats(upper, lower):
    return pl.pallas_call(
        stats_kernel,
        out_shape=jax.ShapeDtypeStruct((STATS, 128), f32),
        grid=(1,),
        in_specs=[whole(), pl.BlockSpec((EDGE, WIDTH, STICKS_DEV), lambda i: (0, 0, 0))],
        out_specs=whole(),
        compiler_params=params(8),
        name="stats",
    )(upper, lower)


def spread_rows(bands, map_ref, pair_ref, out_ref):
    position = map_ref[...]
    kx = sixth(position)
    place = GBOX * (position - GY_DEV * kx) + kx
    select = (lax.broadcasted_iota(jnp.int32, (STICKS_DEV, STICKS_DEV), 0) == place).astype(f32).astype(bf16)
    both = jnp.concatenate(
        [part for re, im in bands for part in (re, im)] + [part for re, im in bands for part in (-im, re)], axis=0
    )
    placed = dot(select, both, NT).astype(bf16)
    for p in range(GY_DEV // 2):
        rows = slice(p * WIDTH, (p + 1) * WIDTH)
        block = jnp.concatenate([placed[rows, :LANES], placed[rows, LANES:]], axis=0)
        result = dot(pair_ref[...], block).astype(bf16)
        out_ref[:, 2 * X_DEV * p : 2 * X_DEV * (p + 1), :] = result.reshape(PENCILS, 2 * X_DEV, LANES)


def ahead_kernel(map_ref, bands_ref, pair_ref, out_ref):
    spread_rows([(bands_ref[b, :GBOX, :], bands_ref[b, GBOX:, :]) for b in range(EDGE)], map_ref, pair_ref, out_ref)


def ahead(position, bands, pair):
    return pl.pallas_call(
        ahead_kernel,
        out_shape=jax.ShapeDtypeStruct((PENCILS, CHUNK, LANES), bf16),
        grid=(1,),
        in_specs=[whole(), pl.BlockSpec((EDGE, WIDTH, STICKS_DEV), lambda i: (1, 0, 0)), whole()],
        out_specs=whole(),
        compiler_params=params(16),
        name="ahead",
    )(position, bands, pair)


def edge_kernel(keep_ref, total_ref, map_ref, bands_ref, upper_ref, pair_ref, out_ref, ortho_ref):
    bands = []
    for i in range(EDGE):
        u_re = bands_ref[i, :GBOX, :].astype(f32)
        u_im = bands_ref[i, GBOX:, :].astype(f32)
        for j in range(EDGE):
            keep = keep_ref[0, i, j].astype(f32)
            divisor = total_ref[8 + j : 9 + j, 0:1] + 1e-05
            w_re = keep * total_ref[2 * j + i : 2 * j + i + 1, 0:1] / divisor
            w_im = keep * total_ref[4 + 2 * j + i : 5 + 2 * j + i, 0:1] / divisor
            p_re = upper_ref[j, :GBOX, :].astype(f32)
            p_im = upper_ref[j, GBOX:, :].astype(f32)
            u_re = u_re - (w_re * p_re - w_im * p_im)
            u_im = u_im - (w_re * p_im + w_im * p_re)
        re, im = u_re.astype(bf16), u_im.astype(bf16)
        ortho_ref[i, :GBOX, :] = re
        ortho_ref[i, GBOX:, :] = im
        bands.append((re, im))
    spread_rows(bands, map_ref, pair_ref, out_ref)


def edge_ahead(keep, total, position, bands, upper, pair):
    return pl.pallas_call(
        edge_kernel,
        out_shape=(
            jax.ShapeDtypeStruct((PENCILS, CHUNK, LANES), bf16),
            jax.ShapeDtypeStruct((EDGE, WIDTH, STICKS_DEV), bf16),
        ),
        grid=(1,),
        in_specs=[
            pl.BlockSpec(memory_space=pltpu.SMEM),
            whole(),
            whole(),
            pl.BlockSpec((EDGE, WIDTH, STICKS_DEV), lambda i: (0, 0, 0)),
            whole(),
            whole(),
        ],
        out_specs=(whole(), whole()),
        compiler_params=params(16),
        name="edge",
    )(keep, total, position, bands, upper, pair)


def grid_kernel(rows_ref, potential_ref, third_ref, second_ref, back_second_ref, back_third_ref, out_ref, wide_ref, back_ref):
    for t in range(3):
        wide_ref[t] = rows_ref[:, :, 128 * t : 128 * t + 128].astype(f32).reshape(ROWS, 128)

    def plane(x, carry):
        rows = pl.ds(x, GBOX, stride=X_DEV)
        section = jnp.concatenate([wide_ref[t, rows, :] for t in range(3)], axis=1).astype(bf16)
        field = potential_ref[x]
        results = []
        for b in range(EDGE):
            lanes = section[:, 128 * b : 128 * b + 256]
            two = dot(lanes, third_ref[b]).astype(bf16)
            stacked = jnp.concatenate([two[:, :GRID], two[:, 256 : 256 + GRID]], axis=0)
            space = dot(second_ref[...], stacked)
            scaled = jnp.concatenate([space[:GRID] * field, space[GRID:] * field], axis=0).astype(bf16)
            one = dot(back_second_ref[...], scaled).astype(bf16)
            results.append(dot(one[:GBOX], back_third_ref[b, :GRID, :]) + dot(one[GBOX:], back_third_ref[b, GRID:, :]))
        back_ref[0, rows, :] = results[0][:, :128]
        back_ref[1, rows, :] = results[0][:, 128:] + results[1][:, :128]
        back_ref[2, rows, :] = results[1][:, 128:]
        return carry

    lax.fori_loop(0, X_DEV, plane, 0)
    for t in range(3):
        out_ref[:, :, 128 * t : 128 * t + 128] = back_ref[t].reshape(PENCILS, CHUNK, 128).astype(bf16)


def on_grid(rows, potential, consts):
    third, second, back_second, back_third = consts
    flops = 2 * EDGE * X_DEV * (96 * 256 * 512 + 384 * 256 * 256 * 2 + 96 * 512 * 256)
    return pl.pallas_call(
        grid_kernel,
        out_shape=jax.ShapeDtypeStruct((PENCILS, CHUNK, LANES), bf16),
        in_specs=[whole()] * 6,
        out_specs=whole(),
        scratch_shapes=[VMEM((3, ROWS, 128), f32), VMEM((3, ROWS, 128), f32)],
        compiler_params=params(16),
        cost_estimate=pl.CostEstimate(flops=flops, bytes_accessed=8_000_000, transcendentals=0),
        name="grid",
    )(rows, potential, third, second, back_second, back_third)


def behind_kernel(map_ref, across_ref, rows_ref, cos_ref, sin_ref, bands_ref, out_ref):
    position = map_ref[...]
    kx = sixth(position)
    gx = (kx - GBOX // 2).astype(f32)
    gy = (position - GY_DEV * kx + GY_DEV * across_ref[0] - GBOX // 2).astype(f32)
    gz = (lax.broadcasted_iota(jnp.int32, (GBOX, STICKS_DEV), 0) - GBOX // 2).astype(f32)
    kinetic = 0.5 * (gx * gx + gy * gy + gz * gz) / float((GBOX // 2) ** 2)
    rows = rows_ref[...].reshape(ROWS, LANES)
    by_cos = dot(rows, cos_ref[...], TN)
    by_sin = dot(rows, sin_ref[...], TN)
    for b in range(EDGE):
        re = slice(b * WIDTH, b * WIDTH + GBOX)
        im = slice(b * WIDTH + GBOX, (b + 1) * WIDTH)
        out_ref[b, :GBOX, :] = (0.5 * (by_cos[re] + by_sin[im]) + kinetic * bands_ref[b, :GBOX, :].astype(f32)).astype(bf16)
        out_ref[b, GBOX:, :] = (0.5 * (by_cos[im] - by_sin[re]) + kinetic * bands_ref[b, GBOX:, :].astype(f32)).astype(bf16)


def behind(position, across, rows, cos, sin, bands, index, partial=None):
    block = (EDGE, WIDTH, STICKS_DEV)
    operands = [position, across, rows, cos, sin, bands]
    in_specs = [
        whole(),
        pl.BlockSpec(memory_space=pltpu.SMEM),
        whole(),
        whole(),
        whole(),
        pl.BlockSpec(block, lambda i: (index, 0, 0)),
    ]
    kernel = behind_kernel
    if partial is not None:
        operands.append(partial)
        in_specs.append(pl.BlockSpec(memory_space=pl.ANY))
        kernel = lambda *refs: behind_kernel(*refs[:6], refs[7])
    return pl.pallas_call(
        kernel,
        out_shape=jax.ShapeDtypeStruct((2 * EDGE, WIDTH, STICKS_DEV), bf16),
        grid=(1,),
        in_specs=in_specs,
        out_specs=pl.BlockSpec(block, lambda i: (index, 0, 0)),
        input_output_aliases={} if partial is None else {6: 0},
        compiler_params=params(16),
        name="behind",
    )(*operands)


def exchange(blocks):
    return lax.all_to_all(blocks, "pencil", split_axis=0, concat_axis=0, tiled=True)


def total_over_pencil(value):
    for bits in ((2, 4, 6), (8, 1, 9)):
        others = [lax.ppermute(value, "pencil", [(i, i ^ bit) for i in range(PENCILS)]) for bit in bits]
        value = (value + others[0]) + (others[1] + others[2])
    return value


def update(wavefunctions, potential, keep_mask, stick_map):
    first, pair, *grid_consts = [jnp.asarray(c) for c in constants()]
    bands = jnp.transpose(wavefunctions, (0, 2, 1))
    slices = lax.axis_size("cuts")
    upper = lax.ppermute(bands[EDGE:], "cuts", [(i, i + 1) for i in range(slices - 1)])
    position = stick_map.reshape(1, STICKS_DEV)
    inner_rows = ahead(position, bands, pair)
    inner_rows = exchange(inner_rows)
    total = total_over_pencil(stats(upper, bands))
    edge_rows, ortho = edge_ahead(keep_mask, total, position, bands, upper, pair)
    edge_rows = exchange(edge_rows)
    cos, sin = build_matrix(position, first)
    inner_back = exchange(on_grid(inner_rows, potential, grid_consts))
    edge_back = exchange(on_grid(edge_rows, potential, grid_consts))
    across = lax.axis_index("pencil").reshape(1).astype(jnp.int32)
    inner_out = behind(position, across, inner_back, cos, sin, bands, 1)
    out = behind(position, across, edge_back, cos, sin, ortho, 0, inner_out)
    return jnp.transpose(out, (0, 2, 1))


def solution(mesh):
    return jax.shard_map(
        update,
        mesh=mesh,
        in_specs=(
            P("cuts", "pencil", None),
            P("pencil", None, None),
            P("cuts", None, None),
            P("pencil"),
        ),
        out_specs=P("cuts", "pencil", None),
        check_vma=False,
    )
```

```python
import math

import jax
import jax.numpy as jnp
import ml_dtypes
import numpy as np
from jax import lax
from jax.experimental import pallas as pl
from jax.experimental.pallas import tpu as pltpu
from jax.sharding import PartitionSpec as P

GRID = 192
EDGE = 2
GBOX = 96
PENCILS = 16
X_DEV = GRID // PENCILS
GY_DEV = GBOX // PENCILS
STICKS_DEV = GBOX * GY_DEV
WIDTH = 2 * GBOX
CHUNK = X_DEV * GY_DEV
ROWS = PENCILS * CHUNK
LANES = EDGE * WIDTH

bf16 = jnp.bfloat16
f32 = jnp.float32
NT = (((1,), (1,)), ((), ()))
TN = (((0,), (0,)), ((), ()))
VMEM = pltpu.VMEM


def tables():
    phases = 2.0 * np.pi / GRID * np.mod(np.outer(np.arange(GBOX) - GBOX // 2, np.arange(GRID)), GRID)
    scale = 1.0 / math.sqrt(GBOX)
    rounded = lambda a: a.astype(np.float32).astype(ml_dtypes.bfloat16).astype(np.float64)
    return rounded(np.cos(phases) * scale), rounded(np.sin(phases) * scale)


def constants():
    cos, sin = tables()
    low = lambda a: np.asarray(a, np.float32).astype(ml_dtypes.bfloat16)
    order = (np.arange(PENCILS)[:, None, None] * X_DEV + np.zeros((1, GY_DEV, 1), int) + np.arange(X_DEV)[None, None, :]).reshape(-1)
    first = np.concatenate([cos.T[order], sin.T[order]], axis=0)
    pair = np.zeros((2, PENCILS, 2, X_DEV, 2, GBOX))
    for k in range(2):
        pair[0, :, k, :, k, :] = cos.T.reshape(PENCILS, X_DEV, GBOX)
        pair[1, :, k, :, k, :] = sin.T.reshape(PENCILS, X_DEV, GBOX)
    pair = np.concatenate(list(pair.reshape(2, 2 * GRID, 2 * GBOX)), axis=1)
    core = np.zeros((WIDTH, 512))
    core[:GBOX, :GRID] = cos
    core[GBOX:, :GRID] = -sin
    core[:GBOX, 256 : 256 + GRID] = sin
    core[GBOX:, 256 : 256 + GRID] = cos
    third = np.zeros((2, 256, 512))
    third[0, :WIDTH] = core
    third[1, 64:] = core
    second = np.block([[cos.T, -sin.T], [sin.T, cos.T]])
    back_second = 0.5 * np.block([[cos, sin], [-sin, cos]])
    back = 0.5 * np.block([[cos.T, -sin.T], [sin.T, cos.T]])
    back_third = np.zeros((2, 2 * GRID, 256))
    back_third[0, :, :WIDTH] = back
    back_third[1, :, 64:] = back
    return [low(a) for a in (first, pair, third, second, back_second, back_third)]


def dot(a, b, dims=None):
    if dims is None:
        return jnp.dot(a, b, preferred_element_type=f32)
    return lax.dot_general(a, b, dims, preferred_element_type=f32)


def whole(*_):
    return pl.BlockSpec(memory_space=VMEM)


def params(mib):
    return pltpu.CompilerParams(vmem_limit_bytes=mib << 20)


def sixth(value):
    return (value * 10923) >> 16


def matrix_kernel(map_ref, first_ref, cos_ref, sin_ref):
    position = map_ref[...]
    kx = sixth(position)
    ky = position - GY_DEV * kx
    select = (lax.broadcasted_iota(jnp.int32, (GBOX, STICKS_DEV), 0) == kx).astype(f32).astype(bf16)
    row = lax.broadcasted_iota(jnp.int32, (CHUNK, STICKS_DEV), 0)
    row_ky = (row * 5462) >> 16
    mask = row_ky == ky
    for part in range(2):
        out_ref = (cos_ref, sin_ref)[part]
        for b in range(PENCILS):
            spread = dot(first_ref[pl.ds(part * ROWS + b * CHUNK, CHUNK), :], select)
            out_ref[pl.ds(b * CHUNK, CHUNK), :] = jnp.where(mask, spread, 0.0).astype(bf16)


def build_matrix(position, first):
    shape = jax.ShapeDtypeStruct((ROWS, STICKS_DEV), bf16)
    return pl.pallas_call(
        matrix_kernel,
        out_shape=(shape, shape),
        in_specs=[whole(), whole()],
        out_specs=(whole(), whole()),
        compiler_params=params(12),
        name="matrix",
    )(position, first)


def start_copy(source, target, sem):
    copy = pltpu.make_async_copy(source, target, sem)
    copy.start()
    return copy


def stats_kernel(upper_ref, lower_ref, _, out_ref, block_ref, sem):
    terms = []
    for j in range(EDGE):
        p_re = upper_ref[j, :GBOX, :].astype(f32)
        p_im = upper_ref[j, GBOX:, :].astype(f32)
        for i in range(EDGE):
            u_re = lower_ref[i, :GBOX, :].astype(f32)
            u_im = lower_ref[i, GBOX:, :].astype(f32)
            terms.append((2 * j + i, jnp.sum(p_re * u_re + p_im * u_im)))
            terms.append((4 + 2 * j + i, jnp.sum(p_re * u_im - p_im * u_re)))
        terms.append((8 + j, jnp.sum(p_re * p_re + p_im * p_im)))
    lane = lax.broadcasted_iota(jnp.int32, (8, LANES), 1)
    row = lax.broadcasted_iota(jnp.int32, (8, LANES), 0)
    value = jnp.zeros((8, LANES), f32)
    for k, term in terms:
        value = jnp.where(lane == k, term, value)
    high = value.astype(bf16).astype(f32)
    middle = (value - high).astype(bf16).astype(f32)
    rest = value - high - middle
    packed = jnp.where(row == 0, high, jnp.where(row == 1, middle, jnp.where(row == 2, rest, 0.0))).astype(bf16)
    block_ref[...] = jnp.broadcast_to(packed[None], (PENCILS, 8, LANES))
    start_copy(block_ref, out_ref.at[:, CHUNK:, :], sem).wait()


def stats(upper, bands, payload):
    return pl.pallas_call(
        stats_kernel,
        out_shape=jax.ShapeDtypeStruct((PENCILS, CHUNK + 8, LANES), bf16),
        grid=(1,),
        in_specs=[
            whole(),
            pl.BlockSpec((EDGE, WIDTH, STICKS_DEV), lambda i: (0, 0, 0)),
            pl.BlockSpec(memory_space=pltpu.HBM),
        ],
        out_specs=pl.BlockSpec(memory_space=pltpu.HBM),
        scratch_shapes=[VMEM((PENCILS, 8, LANES), bf16), pltpu.SemaphoreType.DMA(())],
        input_output_aliases={2: 0},
        compiler_params=params(8),
        name="stats",
    )(upper, bands, payload)


def spread_rows(bands, map_ref, pair_ref, out_ref, block_ref, sems):
    position = map_ref[...]
    kx = sixth(position)
    place = GBOX * (position - GY_DEV * kx) + kx
    select = (lax.broadcasted_iota(jnp.int32, (STICKS_DEV, STICKS_DEV), 0) == place).astype(f32).astype(bf16)
    both = jnp.concatenate(
        [part for re, im in bands for part in (re, im)] + [part for re, im in bands for part in (-im, re)], axis=0
    )
    placed = dot(select, both, NT).astype(bf16)
    copies = []
    for p in range(GY_DEV // 2):
        rows = slice(p * WIDTH, (p + 1) * WIDTH)
        block = jnp.concatenate([placed[rows, :LANES], placed[rows, LANES:]], axis=0)
        result = dot(pair_ref[...], block).astype(bf16)
        block_ref[p] = result.reshape(PENCILS, 2 * X_DEV, LANES)
        copies.append(start_copy(block_ref.at[p], out_ref.at[:, 2 * X_DEV * p : 2 * X_DEV * (p + 1), :], sems.at[p]))
    for copy in copies:
        copy.wait()


def spread_scratch():
    return [VMEM((GY_DEV // 2, PENCILS, 2 * X_DEV, LANES), bf16), pltpu.SemaphoreType.DMA((GY_DEV // 2,))]


def ahead_kernel(map_ref, bands_ref, pair_ref, out_ref, *rest):
    block_ref, sems = rest[-2:]
    bands = [(bands_ref[b, :GBOX, :], bands_ref[b, GBOX:, :]) for b in range(EDGE)]
    spread_rows(bands, map_ref, pair_ref, out_ref, block_ref, sems)


HBM = pl.BlockSpec(memory_space=pltpu.HBM)
ROWS_SHAPE = jax.ShapeDtypeStruct((PENCILS, CHUNK, LANES), bf16)
BANDS_SHAPE = jax.ShapeDtypeStruct((EDGE, WIDTH, STICKS_DEV), bf16)


def ahead(position, bands, pair):
    return pl.pallas_call(
        ahead_kernel,
        out_shape=(jax.ShapeDtypeStruct((PENCILS, CHUNK + 8, LANES), bf16), BANDS_SHAPE, ROWS_SHAPE, ROWS_SHAPE, ROWS_SHAPE),
        grid=(1,),
        in_specs=[whole(), pl.BlockSpec((EDGE, WIDTH, STICKS_DEV), lambda i: (1, 0, 0)), whole()],
        out_specs=(HBM,) * 5,
        scratch_shapes=spread_scratch(),
        compiler_params=params(60),
        name="ahead",
    )(position, bands, pair)


def edge_kernel(keep_ref, sums_ref, map_ref, bands_ref, upper_ref, pair_ref, _, __, out_ref, ortho_out_ref, block_ref, sems, ortho_ref, ortho_sem):
    total = jnp.sum(jnp.sum(sums_ref[...].astype(f32), axis=0), axis=0, keepdims=True)
    bands = []
    for i in range(EDGE):
        u_re = bands_ref[i, :GBOX, :].astype(f32)
        u_im = bands_ref[i, GBOX:, :].astype(f32)
        for j in range(EDGE):
            keep = keep_ref[0, i, j].astype(f32)
            divisor = total[:, 8 + j : 9 + j] + 1e-05
            w_re = keep * total[:, 2 * j + i : 2 * j + i + 1] / divisor
            w_im = keep * total[:, 4 + 2 * j + i : 5 + 2 * j + i] / divisor
            p_re = upper_ref[j, :GBOX, :].astype(f32)
            p_im = upper_ref[j, GBOX:, :].astype(f32)
            u_re = u_re - (w_re * p_re - w_im * p_im)
            u_im = u_im - (w_re * p_im + w_im * p_re)
        re, im = u_re.astype(bf16), u_im.astype(bf16)
        ortho_ref[i, :GBOX, :] = re
        ortho_ref[i, GBOX:, :] = im
        bands.append((re, im))
    copy = start_copy(ortho_ref, ortho_out_ref, ortho_sem)
    spread_rows(bands, map_ref, pair_ref, out_ref, block_ref, sems)
    copy.wait()


def edge_ahead(keep, sums, position, bands, upper, pair, rows_buffer, ortho_buffer):
    return pl.pallas_call(
        edge_kernel,
        out_shape=(ROWS_SHAPE, BANDS_SHAPE),
        grid=(1,),
        in_specs=[
            pl.BlockSpec(memory_space=pltpu.SMEM),
            pl.BlockSpec((PENCILS, 8, LANES), lambda i: (0, CHUNK // 8, 0)),
            whole(),
            pl.BlockSpec((EDGE, WIDTH, STICKS_DEV), lambda i: (0, 0, 0)),
            whole(),
            whole(),
            HBM,
            HBM,
        ],
        out_specs=(HBM, HBM),
        input_output_aliases={6: 0, 7: 1},
        scratch_shapes=spread_scratch() + [VMEM((EDGE, WIDTH, STICKS_DEV), bf16), pltpu.SemaphoreType.DMA(())],
        compiler_params=params(16),
        name="edge",
    )(keep, sums, position, bands, upper, pair, rows_buffer, ortho_buffer)


PARTS = 4
PLANES = 2


def grid_kernel(rows_hbm, potential_hbm, third_hbm, second_hbm, back_second_hbm, back_third_hbm, _, out_hbm, *scratch):
    rows_ref, wide_ref, back_ref, done_ref, potential_ref, third_ref, second_ref, back_second_ref, back_third_ref = scratch[:9]
    row_sems, plane_sems, const_sems, out_sems = scratch[9:]
    group = PENCILS // PARTS
    row_copies = [
        start_copy(rows_hbm.at[group * g : group * (g + 1), :CHUNK, :], rows_ref.at[group * g : group * (g + 1)], row_sems.at[g])
        for g in range(PARTS)
    ]
    consts = ((third_hbm, third_ref), (second_hbm, second_ref), (back_second_hbm, back_second_ref), (back_third_hbm, back_third_ref))
    const_copies = [start_copy(source, target, const_sems.at[k]) for k, (source, target) in enumerate(consts)]
    for x in range(X_DEV):
        start_copy(potential_hbm.at[x], potential_ref.at[x], plane_sems.at[x])
    span = group * CHUNK
    for g in range(PARTS):
        row_copies[g].wait()
        block = rows_ref[group * g : group * (g + 1)]
        for t in range(3):
            wide_ref[t, span * g : span * (g + 1), :] = block[:, :, 128 * t : 128 * t + 128].astype(f32).reshape(span, 128)
    for copy in const_copies:
        copy.wait()

    def planes(step, carry):
        for u in range(PLANES):
            x = PLANES * step + u
            pltpu.make_async_copy(potential_hbm.at[x], potential_ref.at[x], plane_sems.at[x]).wait()
        work = []
        for u in range(PLANES):
            x = PLANES * step + u
            rows = pl.ds(x, GBOX, stride=X_DEV)
            section = jnp.concatenate([wide_ref[t, rows, :] for t in range(3)], axis=1).astype(bf16)
            field = potential_ref[x]
            results = []
            for b in range(EDGE):
                two = dot(section[:, 128 * b : 128 * b + 256], third_ref[b]).astype(bf16)
                stacked = jnp.concatenate([two[:, :GRID], two[:, 256 : 256 + GRID]], axis=0)
                space = dot(second_ref[...], stacked)
                scaled = jnp.concatenate([space[:GRID] * field, space[GRID:] * field], axis=0).astype(bf16)
                one = dot(back_second_ref[...], scaled).astype(bf16)
                results.append(dot(one[:GBOX], back_third_ref[b, :GRID, :]) + dot(one[GBOX:], back_third_ref[b, GRID:, :]))
            work.append((rows, results))
        for rows, results in work:
            back_ref[0, rows, :] = results[0][:, :128]
            back_ref[1, rows, :] = results[0][:, 128:] + results[1][:, :128]
            back_ref[2, rows, :] = results[1][:, 128:]
        return carry

    lax.fori_loop(0, X_DEV // PLANES, planes, 0)
    out_copies = []
    for g in range(PARTS):
        for t in range(3):
            part = back_ref[t, span * g : span * (g + 1), :].reshape(group, CHUNK, 128)
            done_ref[group * g : group * (g + 1), :, 128 * t : 128 * t + 128] = part.astype(bf16)
        out_copies.append(
            start_copy(done_ref.at[group * g : group * (g + 1)], out_hbm.at[group * g : group * (g + 1)], out_sems.at[g])
        )
    for copy in out_copies:
        copy.wait()


def on_grid(rows, potential, consts, buffer):
    flops = 2 * EDGE * X_DEV * (96 * 256 * 512 + 384 * 256 * 256 * 2 + 96 * 512 * 256)
    third, second, back_second, back_third = consts
    DMA = pltpu.SemaphoreType.DMA
    return pl.pallas_call(
        grid_kernel,
        out_shape=ROWS_SHAPE,
        in_specs=[HBM] * 7,
        out_specs=HBM,
        input_output_aliases={6: 0},
        scratch_shapes=[
            VMEM((PENCILS, CHUNK, LANES), bf16),
            VMEM((3, ROWS, 128), f32),
            VMEM((3, ROWS, 128), f32),
            VMEM((PENCILS, CHUNK, LANES), bf16),
            VMEM((X_DEV, GRID, GRID), f32),
            VMEM(third.shape, bf16),
            VMEM(second.shape, bf16),
            VMEM(back_second.shape, bf16),
            VMEM(back_third.shape, bf16),
            DMA((PARTS,)),
            DMA((X_DEV,)),
            DMA((4,)),
            DMA((PARTS,)),
        ],
        compiler_params=params(60),
        cost_estimate=pl.CostEstimate(flops=flops, bytes_accessed=8_000_000, transcendentals=0),
        name="grid",
    )(rows, potential, *consts, buffer)


def behind_kernel(map_ref, across_ref, rows_ref, cos_ref, sin_ref, bands_ref, out_ref):
    position = map_ref[...]
    kx = sixth(position)
    gx = (kx - GBOX // 2).astype(f32)
    gy = (position - GY_DEV * kx + GY_DEV * across_ref[0] - GBOX // 2).astype(f32)
    gz = (lax.broadcasted_iota(jnp.int32, (GBOX, STICKS_DEV), 0) - GBOX // 2).astype(f32)
    kinetic = 0.5 * (gx * gx + gy * gy + gz * gz) / float((GBOX // 2) ** 2)
    rows = rows_ref[...].reshape(ROWS, LANES)
    by_cos = dot(rows, cos_ref[...], TN)
    by_sin = dot(rows, sin_ref[...], TN)
    for b in range(EDGE):
        re = slice(b * WIDTH, b * WIDTH + GBOX)
        im = slice(b * WIDTH + GBOX, (b + 1) * WIDTH)
        out_ref[b, :GBOX, :] = (0.5 * (by_cos[re] + by_sin[im]) + kinetic * bands_ref[b, :GBOX, :].astype(f32)).astype(bf16)
        out_ref[b, GBOX:, :] = (0.5 * (by_cos[im] - by_sin[re]) + kinetic * bands_ref[b, GBOX:, :].astype(f32)).astype(bf16)


def behind(position, across, rows, cos, sin, bands, index, partial=None):
    block = (EDGE, WIDTH, STICKS_DEV)
    operands = [position, across, rows, cos, sin, bands]
    in_specs = [
        whole(),
        pl.BlockSpec(memory_space=pltpu.SMEM),
        whole(),
        whole(),
        whole(),
        pl.BlockSpec(block, lambda i: (index, 0, 0)),
    ]
    kernel = behind_kernel
    if partial is not None:
        operands.append(partial)
        in_specs.append(pl.BlockSpec(memory_space=pl.ANY))
        kernel = lambda *refs: behind_kernel(*refs[:6], refs[7])
    return pl.pallas_call(
        kernel,
        out_shape=jax.ShapeDtypeStruct((2 * EDGE, WIDTH, STICKS_DEV), bf16),
        grid=(1,),
        in_specs=in_specs,
        out_specs=pl.BlockSpec(block, lambda i: (index, 0, 0)),
        input_output_aliases={} if partial is None else {6: 0},
        compiler_params=params(16),
        name="behind",
    )(*operands)


def exchange(blocks):
    return lax.all_to_all(blocks, "pencil", split_axis=0, concat_axis=0, tiled=True)


def update(wavefunctions, potential, keep_mask, stick_map):
    first, pair, *grid_consts = [jnp.asarray(c) for c in constants()]
    bands = jnp.transpose(wavefunctions, (0, 2, 1))
    slices = lax.axis_size("cuts")
    upper = lax.ppermute(bands[EDGE:], "cuts", [(i, i + 1) for i in range(slices - 1)])
    position = stick_map.reshape(1, STICKS_DEV)
    inner_rows, ortho, edge_rows, inner_buffer, edge_buffer = ahead(position, bands, pair)
    inner_rows = exchange(stats(upper, bands, inner_rows))
    edge_rows, ortho = edge_ahead(keep_mask, inner_rows, position, bands, upper, pair, edge_rows, ortho)
    edge_rows = exchange(edge_rows)
    cos, sin = build_matrix(position, first)
    inner_back = exchange(on_grid(inner_rows, potential, grid_consts, inner_buffer))
    edge_back = exchange(on_grid(edge_rows, potential, grid_consts, edge_buffer))
    across = lax.axis_index("pencil").reshape(1).astype(jnp.int32)
    inner_out = behind(position, across, inner_back, cos, sin, bands, 1)
    out = behind(position, across, edge_back, cos, sin, ortho, 0, inner_out)
    return jnp.transpose(out, (0, 2, 1))


def solution(mesh):
    return jax.shard_map(
        update,
        mesh=mesh,
        in_specs=(
            P("cuts", "pencil", None),
            P("pencil", None, None),
            P("cuts", None, None),
            P("pencil"),
        ),
        out_specs=P("cuts", "pencil", None),
        check_vma=False,
    )
```

```python
import math

import jax
import jax.numpy as jnp
import ml_dtypes
import numpy as np
from jax import lax
from jax.experimental import pallas as pl
from jax.experimental.pallas import tpu as pltpu
from jax.sharding import PartitionSpec as P

GRID = 192
EDGE = 2
GBOX = 96
PENCILS = 16
X_DEV = GRID // PENCILS
GY_DEV = GBOX // PENCILS
STICKS_DEV = GBOX * GY_DEV
WIDTH = 2 * GBOX
CHUNK = X_DEV * GY_DEV
ROWS = PENCILS * CHUNK
LANES = EDGE * WIDTH
PARTS = 4
GROUPS = 2
STAGGER_NS = 2500

bf16 = jnp.bfloat16
f32 = jnp.float32
NT = (((1,), (1,)), ((), ()))
TN = (((0,), (0,)), ((), ()))
VMEM = pltpu.VMEM


def tables():
    phases = 2.0 * np.pi / GRID * np.mod(np.outer(np.arange(GBOX) - GBOX // 2, np.arange(GRID)), GRID)
    scale = 1.0 / math.sqrt(GBOX)
    rounded = lambda a: a.astype(np.float32).astype(ml_dtypes.bfloat16).astype(np.float64)
    return rounded(np.cos(phases) * scale), rounded(np.sin(phases) * scale)


def constants():
    cos, sin = tables()
    low = lambda a: np.asarray(a, np.float32).astype(ml_dtypes.bfloat16)
    pair = np.zeros((2, PENCILS, 2, X_DEV, 2, GBOX))
    for k in range(2):
        pair[0, :, k, :, k, :] = cos.T.reshape(PENCILS, X_DEV, GBOX)
        pair[1, :, k, :, k, :] = sin.T.reshape(PENCILS, X_DEV, GBOX)
    halves = pair.reshape(2, 2 * GRID, 2 * GBOX)
    pair = np.concatenate(list(halves), axis=1)
    core = np.zeros((WIDTH, 512))
    core[:GBOX, :GRID] = cos
    core[GBOX:, :GRID] = -sin
    core[:GBOX, 256 : 256 + GRID] = sin
    core[GBOX:, 256 : 256 + GRID] = cos
    third = np.zeros((2, 256, 512))
    third[0, :WIDTH] = core
    third[1, 64:] = core
    second = np.block([[cos.T, -sin.T], [sin.T, cos.T]])
    back_second = 0.5 * np.block([[cos, sin], [-sin, cos]])
    back = 0.5 * np.block([[cos.T, -sin.T], [sin.T, cos.T]])
    back_third = np.zeros((2, 2 * GRID, 256))
    back_third[0, :, :WIDTH] = back
    back_third[1, :, 64:] = back
    return [low(a) for a in (pair, halves, third, second, back_second, back_third)]


def dot(a, b, dims=None):
    if dims is None:
        return jnp.dot(a, b, preferred_element_type=f32)
    return lax.dot_general(a, b, dims, preferred_element_type=f32)


def whole(*_):
    return pl.BlockSpec(memory_space=VMEM)


def params(mib):
    return pltpu.CompilerParams(vmem_limit_bytes=mib << 20)


def sixth(value):
    return (value * 10923) >> 16


def positions(map_ref):
    position = map_ref[...].reshape(1, STICKS_DEV)
    kx = sixth(position)
    return kx, position - GY_DEV * kx


def placing(map_ref):
    kx, ky = positions(map_ref)
    place = GBOX * ky + kx
    return (lax.broadcasted_iota(jnp.int32, (STICKS_DEV, STICKS_DEV), 0) == place).astype(f32).astype(bf16)


def start_copy(source, target, sem):
    copy = pltpu.make_async_copy(source, target, sem)
    copy.start()
    return copy


def own_sums(place_ref, upper_ref, lower_ref, block_ref):
    terms = []
    for j in range(EDGE):
        p_re = upper_ref[j, :GBOX, :].astype(f32)
        p_im = upper_ref[j, GBOX:, :].astype(f32)
        for i in range(EDGE):
            u_re = lower_ref[i, :GBOX, :].astype(f32)
            u_im = lower_ref[i, GBOX:, :].astype(f32)
            terms.append((2 * j + i, jnp.sum(p_re * u_re + p_im * u_im)))
            terms.append((4 + 2 * j + i, jnp.sum(p_re * u_im - p_im * u_re)))
        terms.append((8 + j, jnp.sum(p_re * p_re + p_im * p_im)))
    lane = lax.broadcasted_iota(jnp.int32, (8, LANES), 1)
    row = lax.broadcasted_iota(jnp.int32, (8, LANES), 0)
    value = jnp.zeros((8, LANES), f32)
    for k, term in terms:
        value = jnp.where(lane == k, term, value)
    value = jnp.where(place_ref[0] > 0, value, 0.0)
    high = value.astype(bf16).astype(f32)
    middle = (value - high).astype(bf16).astype(f32)
    rest = value - high - middle
    packed = jnp.where(row == 0, high, jnp.where(row == 1, middle, jnp.where(row == 2, rest, 0.0))).astype(bf16)
    block_ref[...] = jnp.broadcast_to(packed[None], (PENCILS, 8, LANES))


def spread_rows(bands, map_ref, pair_ref, out_ref, block_ref, sems):
    both = jnp.concatenate(
        [part for re, im in bands for part in (re, im)] + [part for re, im in bands for part in (-im, re)], axis=0
    )
    placed = dot(placing(map_ref), both, NT).astype(bf16)
    copies = []
    for p in range(GY_DEV // 2):
        rows = slice(p * WIDTH, (p + 1) * WIDTH)
        block = jnp.concatenate([placed[rows, :LANES], placed[rows, LANES:]], axis=0)
        result = dot(pair_ref[...], block).astype(bf16)
        block_ref[p] = result.reshape(PENCILS, 2 * X_DEV, LANES)
        copies.append(start_copy(block_ref.at[p], out_ref.at[:, 2 * X_DEV * p : 2 * X_DEV * (p + 1), :], sems.at[p]))
    for copy in copies:
        copy.wait()


def spread_scratch():
    return [VMEM((GY_DEV // 2, PENCILS, 2 * X_DEV, LANES), bf16), pltpu.SemaphoreType.DMA((GY_DEV // 2,))]


def ahead_kernel(place_ref, map_ref, bands_ref, upper_ref, pair_ref, out_ref, *rest):
    block_ref, sems, sums_ref, sums_sem = rest[-4:]
    own_sums(place_ref, upper_ref, bands_ref.at[:EDGE], sums_ref)
    copy = start_copy(sums_ref, out_ref.at[:, CHUNK:, :], sums_sem)
    bands = [(bands_ref[b, :GBOX, :], bands_ref[b, GBOX:, :]) for b in range(EDGE, 2 * EDGE)]
    spread_rows(bands, map_ref, pair_ref, out_ref, block_ref, sems)
    copy.wait()

    @pl.when(place_ref[0] % 2 == 0)
    def _():
        pl.delay(STAGGER_NS)


HBM = pl.BlockSpec(memory_space=pltpu.HBM)
ROWS_SHAPE = jax.ShapeDtypeStruct((PENCILS, CHUNK, LANES), bf16)
BANDS_SHAPE = jax.ShapeDtypeStruct((EDGE, WIDTH, STICKS_DEV), bf16)


def ahead(place, position, bands, upper, pair):
    return pl.pallas_call(
        ahead_kernel,
        out_shape=(jax.ShapeDtypeStruct((PENCILS, CHUNK + 8, LANES), bf16), BANDS_SHAPE, ROWS_SHAPE, ROWS_SHAPE, ROWS_SHAPE),
        grid=(1,),
        in_specs=[pl.BlockSpec(memory_space=pltpu.SMEM)] + [whole()] * 4,
        out_specs=(HBM,) * 5,
        scratch_shapes=spread_scratch() + [VMEM((PENCILS, 8, LANES), bf16), pltpu.SemaphoreType.DMA(())],
        compiler_params=params(60),
        name="ahead",
    )(place, position, bands, upper, pair)


def edge_kernel(place_ref, keep_ref, sums_ref, map_ref, bands_ref, upper_ref, pair_ref, _, __, out_ref, ortho_out_ref, block_ref, sems, ortho_ref, ortho_sem):
    total = jnp.sum(jnp.sum(sums_ref[...].astype(f32), axis=0), axis=0, keepdims=True)
    bands = []
    for i in range(EDGE):
        u_re = bands_ref[i, :GBOX, :].astype(f32)
        u_im = bands_ref[i, GBOX:, :].astype(f32)
        for j in range(EDGE):
            keep = jnp.where(place_ref[0] > 0, keep_ref[0, i, j].astype(f32), 0.0)
            divisor = total[:, 8 + j : 9 + j] + 1e-05
            w_re = keep * total[:, 2 * j + i : 2 * j + i + 1] / divisor
            w_im = keep * total[:, 4 + 2 * j + i : 5 + 2 * j + i] / divisor
            p_re = upper_ref[j, :GBOX, :].astype(f32)
            p_im = upper_ref[j, GBOX:, :].astype(f32)
            u_re = u_re - (w_re * p_re - w_im * p_im)
            u_im = u_im - (w_re * p_im + w_im * p_re)
        re, im = u_re.astype(bf16), u_im.astype(bf16)
        ortho_ref[i, :GBOX, :] = re
        ortho_ref[i, GBOX:, :] = im
        bands.append((re, im))
    copy = start_copy(ortho_ref, ortho_out_ref, ortho_sem)
    spread_rows(bands, map_ref, pair_ref, out_ref, block_ref, sems)
    copy.wait()


def edge_ahead(place, keep, sums, position, bands, upper, pair, rows_buffer, ortho_buffer):
    return pl.pallas_call(
        edge_kernel,
        out_shape=(ROWS_SHAPE, BANDS_SHAPE),
        grid=(1,),
        in_specs=[
            pl.BlockSpec(memory_space=pltpu.SMEM),
            pl.BlockSpec(memory_space=pltpu.SMEM),
            pl.BlockSpec((PENCILS, 8, LANES), lambda i: (0, CHUNK // 8, 0)),
            whole(),
            pl.BlockSpec((EDGE, WIDTH, STICKS_DEV), lambda i: (0, 0, 0)),
            whole(),
            whole(),
            HBM,
            HBM,
        ],
        out_specs=(HBM, HBM),
        input_output_aliases={7: 0, 8: 1},
        scratch_shapes=spread_scratch() + [VMEM((EDGE, WIDTH, STICKS_DEV), bf16), pltpu.SemaphoreType.DMA(())],
        compiler_params=params(16),
        name="edge",
    )(place, keep, sums, position, bands, upper, pair, rows_buffer, ortho_buffer)


def grid_kernel(rows_hbm, potential_hbm, third_hbm, second_hbm, back_second_hbm, back_third_hbm, _, out_hbm, *scratch):
    rows_ref, wide_ref, back_ref, done_ref, potential_ref, third_ref, second_ref, back_second_ref, back_third_ref = scratch[:9]
    row_sems, plane_sems, const_sems, out_sems = scratch[9:]
    group = PENCILS // PARTS
    row_copies = [
        start_copy(rows_hbm.at[group * g : group * (g + 1), :CHUNK, :], rows_ref.at[group * g : group * (g + 1)], row_sems.at[g])
        for g in range(PARTS)
    ]
    consts = ((third_hbm, third_ref), (second_hbm, second_ref), (back_second_hbm, back_second_ref), (back_third_hbm, back_third_ref))
    const_copies = [start_copy(source, target, const_sems.at[k]) for k, (source, target) in enumerate(consts)]
    span = group * CHUNK
    for g in range(PARTS):
        row_copies[g].wait()
        block = rows_ref[group * g : group * (g + 1)]
        for t in range(3):
            wide_ref[t, span * g : span * (g + 1), :] = block[:, :, 128 * t : 128 * t + 128].astype(f32).reshape(span, 128)
        for x in range(g * X_DEV // PARTS, (g + 1) * X_DEV // PARTS):
            start_copy(potential_hbm.at[x], potential_ref.at[x], plane_sems.at[x])
    planes = X_DEV // GROUPS
    const_copies[0].wait()

    def group_of_planes(h, carry):
        strides = [pl.ds(planes * h + u, GBOX, stride=X_DEV) for u in range(planes)]
        section = jnp.concatenate(
            [jnp.concatenate([wide_ref[t, rows, :] for t in range(3)], axis=1).astype(bf16) for rows in strides], axis=0
        )
        twos = [dot(section[:, 128 * b : 128 * b + 256], third_ref[b]).astype(bf16) for b in range(EDGE)]

        @pl.when(h == 0)
        def _():
            for copy in const_copies[1:]:
                copy.wait()

        for u in range(planes):
            x = planes * h + u
            pltpu.make_async_copy(potential_hbm.at[x], potential_ref.at[x], plane_sems.at[x]).wait()
        results = []
        for b in range(EDGE):
            ones = []
            for u in range(planes):
                field = potential_ref[planes * h + u]
                own = slice(GBOX * u, GBOX * (u + 1))
                stacked = jnp.concatenate([twos[b][own, :GRID], twos[b][own, 256 : 256 + GRID]], axis=0)
                space = dot(second_ref[...], stacked)
                scaled = jnp.concatenate([space[:GRID] * field, space[GRID:] * field], axis=0).astype(bf16)
                ones.append(dot(back_second_ref[...], scaled).astype(bf16))
            real = jnp.concatenate([one[:GBOX] for one in ones], axis=0)
            imag = jnp.concatenate([one[GBOX:] for one in ones], axis=0)
            results.append(dot(real, back_third_ref[b, :GRID, :]) + dot(imag, back_third_ref[b, GRID:, :]))
        for u, rows in enumerate(strides):
            own = slice(GBOX * u, GBOX * (u + 1))
            back_ref[0, rows, :] = results[0][own, :128]
            back_ref[1, rows, :] = results[0][own, 128:] + results[1][own, :128]
            back_ref[2, rows, :] = results[1][own, 128:]
        return carry

    lax.fori_loop(0, GROUPS, group_of_planes, 0)
    out_copies = []
    for g in range(PARTS):
        for t in range(3):
            part = back_ref[t, span * g : span * (g + 1), :].reshape(group, CHUNK, 128)
            done_ref[group * g : group * (g + 1), :, 128 * t : 128 * t + 128] = part.astype(bf16)
        out_copies.append(
            start_copy(done_ref.at[group * g : group * (g + 1)], out_hbm.at[group * g : group * (g + 1)], out_sems.at[g])
        )
    for copy in out_copies:
        copy.wait()


def on_grid(rows, potential, consts, buffer):
    flops = 2 * EDGE * X_DEV * (96 * 256 * 512 + 384 * 256 * 256 * 2 + 96 * 512 * 256)
    third, second, back_second, back_third = consts
    DMA = pltpu.SemaphoreType.DMA
    return pl.pallas_call(
        grid_kernel,
        out_shape=ROWS_SHAPE,
        in_specs=[HBM] * 7,
        out_specs=HBM,
        input_output_aliases={6: 0},
        scratch_shapes=[
            VMEM((PENCILS, CHUNK, LANES), bf16),
            VMEM((3, ROWS, 128), f32),
            VMEM((3, ROWS, 128), f32),
            VMEM((PENCILS, CHUNK, LANES), bf16),
            VMEM((X_DEV, GRID, GRID), f32),
            VMEM(third.shape, bf16),
            VMEM(second.shape, bf16),
            VMEM(back_second.shape, bf16),
            VMEM(back_third.shape, bf16),
            DMA((PARTS,)),
            DMA((X_DEV,)),
            DMA((4,)),
            DMA((PARTS,)),
        ],
        compiler_params=params(60),
        cost_estimate=pl.CostEstimate(flops=flops, bytes_accessed=8_000_000, transcendentals=0),
        name="grid",
    )(rows, potential, *consts, buffer)


def behind_kernel(map_ref, across_ref, rows_ref, halves_ref, bands_ref, out_ref):
    kx, ky = positions(map_ref)
    gx = (kx - GBOX // 2).astype(f32)
    gy = (ky + GY_DEV * across_ref[0] - GBOX // 2).astype(f32)
    gz = (lax.broadcasted_iota(jnp.int32, (GBOX, STICKS_DEV), 0) - GBOX // 2).astype(f32)
    kinetic = 0.5 * (gx * gx + gy * gy + gz * gz) / float((GBOX // 2) ** 2)
    select = placing(map_ref)
    sums = None
    for p in range(GY_DEV // 2):
        rows = rows_ref[:, 2 * X_DEV * p : 2 * X_DEV * (p + 1), :].reshape(2 * GRID, LANES)
        by_cos = dot(rows, halves_ref[0], TN)
        by_sin = dot(rows, halves_ref[1], TN)
        parts = []
        for b in range(EDGE):
            re = slice(b * WIDTH, b * WIDTH + GBOX)
            im = slice(b * WIDTH + GBOX, (b + 1) * WIDTH)
            parts += [0.5 * (by_cos[re] + by_sin[im]), 0.5 * (by_cos[im] - by_sin[re])]
        term = dot(jnp.concatenate(parts, axis=0).astype(bf16), select[WIDTH * p : WIDTH * (p + 1)])
        sums = term if sums is None else sums + term
    for b in range(EDGE):
        for h in range(2):
            own = bands_ref[b, GBOX * h : GBOX * (h + 1), :].astype(f32)
            base = b * WIDTH + h * GBOX
            out_ref[b, GBOX * h : GBOX * (h + 1), :] = (sums[base : base + GBOX] + kinetic * own).astype(bf16)


def behind(position, across, rows, halves, bands, index, partial=None):
    block = (EDGE, WIDTH, STICKS_DEV)
    operands = [position, across, rows, halves, bands]
    in_specs = [
        whole(),
        pl.BlockSpec(memory_space=pltpu.SMEM),
        whole(),
        whole(),
        pl.BlockSpec(block, lambda i: (index, 0, 0)),
    ]
    kernel = behind_kernel
    if partial is not None:
        operands.append(partial)
        in_specs.append(pl.BlockSpec(memory_space=pl.ANY))
        kernel = lambda *refs: behind_kernel(*refs[:5], refs[6])
    return pl.pallas_call(
        kernel,
        out_shape=jax.ShapeDtypeStruct((2 * EDGE, WIDTH, STICKS_DEV), bf16),
        grid=(1,),
        in_specs=in_specs,
        out_specs=pl.BlockSpec(block, lambda i: (index, 0, 0)),
        input_output_aliases={} if partial is None else {5: 0},
        compiler_params=params(16),
        name="behind",
    )(*operands)


def exchange(blocks):
    return lax.all_to_all(blocks, "pencil", split_axis=0, concat_axis=0, tiled=True)


def local(wavefunctions, potential, keep_mask, stick_map):
    pair, halves, *grid_consts = [jnp.asarray(c) for c in constants()]
    bands = jnp.transpose(wavefunctions, (0, 2, 1))
    slices = lax.axis_size("cuts")
    upper = lax.ppermute(bands[EDGE:], "cuts", [(i, (i + 1) % slices) for i in range(slices)])
    place = lax.axis_index("cuts").reshape(1).astype(jnp.int32)
    inner_rows, ortho, edge_rows, inner_buffer, edge_buffer = ahead(place, stick_map, bands, upper, pair)
    inner_rows = exchange(inner_rows)
    edge_rows, ortho = edge_ahead(place, keep_mask, inner_rows, stick_map, bands, upper, pair, edge_rows, ortho)
    edge_rows = exchange(edge_rows)
    inner_back = exchange(on_grid(inner_rows, potential, grid_consts, inner_buffer))
    edge_back = exchange(on_grid(edge_rows, potential, grid_consts, edge_buffer))
    across = lax.axis_index("pencil").reshape(1).astype(jnp.int32)
    inner_out = behind(stick_map, across, inner_back, halves, bands, 1)
    out = behind(stick_map, across, edge_back, halves, ortho, 0, inner_out)
    return jnp.transpose(out, (0, 2, 1))


def solution(mesh):
    return jax.shard_map(
        local,
        mesh=mesh,
        in_specs=(
            P("cuts", "pencil", None),
            P("pencil", None, None),
            P("cuts", None, None),
            P("pencil"),
        ),
        out_specs=P("cuts", "pencil", None),
        check_vma=False,
    )
```
